32 devices in a mesh: samp: 16 (over z, x, core), var: 2 (over y).
Axes of the slice: x: 2, y: 2, z: 4, core: 2. Of those that a mesh axis runs over, the one named last changes fastest.
Arguments:
- genotypes: bfloat16 [16384, 12288], P('samp', 'var'), may hold values from 0 to 2, as said below
- start_q: float32 [64, 16384], P(None, 'samp'), may hold values from 0 to 1, as said below
Outputs:
- final_q: float32 [64, 16384], P(None, 'samp')
- final_p: float32 [64, 12288], P(None, 'var')
The draws below stay inside these ranges and needn't reach their ends.
Inputs may be any that keep to these rules, and one draw needn't show every extreme that they name: `genotypes`: genotype counts, whole numbers. `start_q`: nonnegative proportions.
All inputs are finite; a program needn't handle non-finite values.
Results may differ from the reference program's by a relative error of at most 0.001.
Values sent between devices are 32-bit elements; how exact they have to be, the bound alone decides.
No kernel may reach another device: no remote copies, remote signals or barrier semaphores. Data moves between devices by JAX's collectives and lax.ppermute only.
A program may use at most 64 MiB of HBM per device.

```python
import jax
import jax.numpy as jnp
from jax import lax

K = 64
VARIANTS = 12288
ITERS = 2
SAMPLES = 16384


def shared_labels(key):
    return jax.random.randint(jax.random.fold_in(key, 7), (SAMPLES,), 0, K)


def draw_genotypes(key, part):
    labels = shared_labels(key)
    pattern = jax.random.randint(jax.random.fold_in(key, 8), (K, VARIANTS), 0, 3)
    noise_part = jax.random.randint(jax.random.fold_in(key, 9), (SAMPLES, VARIANTS), 0, 3)
    keep_mask = jax.random.randint(jax.random.fold_in(key, 10), (SAMPLES, VARIANTS), 0, 2)
    counts = jnp.where(keep_mask == 1, pattern[labels], noise_part)
    return counts.astype(jnp.bfloat16)


def draw_start_q(key, part):
    labels = shared_labels(key)
    onehot = (jnp.arange(K)[:, None] == labels[None, :]).astype(jnp.float32)
    noise_part = jax.random.uniform(jax.random.fold_in(key, 12), (K, SAMPLES), jnp.float32)
    return 0.6 * onehot + 0.4 * noise_part


def setup_inputs(seed: int = 0) -> dict:
    keys = jax.random.split(jax.random.key(seed), 3)
    return {
        "genotypes": draw_genotypes(jax.random.fold_in(keys[2], 71), 0),
        "start_q": draw_start_q(jax.random.fold_in(keys[2], 71), 0),
    }


ridge_term = 1.0

def gram_solve(gram_matrix, right_side):
    eye_matrix = jnp.eye(gram_matrix.shape[0], dtype=jnp.float32)
    factor_low = jnp.linalg.cholesky(gram_matrix + ridge_term * eye_matrix)
    return jax.scipy.linalg.cho_solve((factor_low, True), right_side)

def reference(genotypes, start_q):
    halved = genotypes * jnp.asarray(0.5, dtype=genotypes.dtype)
    ancestry = start_q
    frequency = None
    for iteration in range(ITERS):
        ancestry_b = ancestry.astype(genotypes.dtype)
        cross_p = jnp.dot(ancestry_b.astype(jnp.float32), halved.astype(jnp.float32), preferred_element_type=jnp.float32)
        gram_q = jnp.dot(ancestry, ancestry.T, precision=lax.Precision.HIGHEST)
        frequency = gram_solve(gram_q, cross_p)
        freq_b = frequency.astype(genotypes.dtype)
        cross_q = lax.dot_general(freq_b.astype(jnp.float32), halved.astype(jnp.float32), (((1,), (1,)), ((), ())), preferred_element_type=jnp.float32)
        gram_p = jnp.dot(frequency, frequency.T, precision=lax.Precision.HIGHEST)
        ancestry = gram_solve(gram_p, cross_q)
    return (ancestry, frequency)
```

```python
import functools

import jax
import jax.numpy as jnp
from jax import lax
from jax.experimental import pallas as pl
from jax.experimental.pallas import tpu as pltpu
from jax.sharding import PartitionSpec as P

ITERS = 2
RIDGE = 1.0
HIGHEST = lax.Precision.HIGHEST


def split_samp(n):
    core = 2 if n % 2 == 0 else 1
    rest = n // core
    inner = max(d for d in range(1, rest + 1) if rest % d == 0 and d * d <= rest)
    return rest // inner, inner, core


def shift_perm(sizes, stage, shift):
    nz, nx, nc = sizes
    pairs = []
    for z in range(nz):
        for x in range(nx):
            for c in range(nc):
                to = [z, x, c]
                to[stage] = (to[stage] + shift) % sizes[stage]
                pairs.append(((z * nx + x) * nc + c, (to[0] * nx + to[1]) * nc + to[2]))
    return pairs


def cross_kernel(nz, n_extra, pos_ref, anc_ref, geno_ref, *refs):
    extra, out_ref, acc_ref = refs[:n_extra], refs[n_extra], refs[n_extra + 1]
    step = pl.program_id(0)
    part = jnp.dot(
        anc_ref[...].astype(jnp.bfloat16), geno_ref[...], preferred_element_type=jnp.float32
    )

    @pl.when(step == 0)
    def _():
        acc_ref[...] = part

    @pl.when(step > 0)
    def _():
        acc_ref[...] += part

    @pl.when(step == pl.num_programs(0) - 1)
    def _():
        chunk = out_ref.shape[2]
        for z in range(nz):
            rel = lax.rem(z - pos_ref[1] + nz, nz)
            value = acc_ref[:, z * chunk : (z + 1) * chunk] * 0.5
            for ref in extra:
                value += ref[rel]
            out_ref[rel] = value


def cross_part(ancestry, genotypes, group, z, nz, groups, extra=()):
    pops, samples = ancestry.shape
    width = genotypes.shape[1] // groups
    chunk = width // nz
    if chunk % 128 or samples % 512:
        part = jnp.dot(
            ancestry.astype(jnp.bfloat16),
            lax.dynamic_slice_in_dim(genotypes, group * width, width, 1),
            preferred_element_type=jnp.float32,
        )
        part = jnp.transpose((part * 0.5).reshape(pops, nz, chunk), (1, 0, 2))
        part = jnp.roll(part, -z, axis=0)
        return functools.reduce(jnp.add, extra, part)
    rows = samples // 4
    whole = pl.BlockSpec((nz, pops, chunk), lambda k, pos: (0, 0, 0))
    return pl.pallas_call(
        functools.partial(cross_kernel, nz, len(extra)),
        out_shape=jax.ShapeDtypeStruct((nz, pops, chunk), jnp.float32),
        grid_spec=pltpu.PrefetchScalarGridSpec(
            num_scalar_prefetch=1,
            grid=(samples // rows,),
            in_specs=[
                pl.BlockSpec((pops, rows), lambda k, pos: (0, k)),
                pl.BlockSpec((rows, width), lambda k, pos: (k, pos[0])),
            ]
            + [whole] * len(extra),
            out_specs=whole,
            scratch_shapes=[pltpu.VMEM((pops, width), jnp.float32)],
        ),
        cost_estimate=pl.CostEstimate(
            flops=2 * pops * samples * width, bytes_accessed=2 * samples * width, transcendentals=0
        ),
        compiler_params=pltpu.CompilerParams(vmem_limit_bytes=16 << 20),
        name="cross_p",
    )(jnp.stack([group, z]).astype(jnp.int32), ancestry, genotypes, *extra)


def fit_kernel(nz, has_acc, pos_ref, freq_ref, geno_ref, *refs):
    if has_acc:
        acc_ref, gacc_ref, out_ref, gram_ref, turned_ref = refs
    else:
        out_ref, gram_ref, turned_ref = refs
    chunk = freq_ref.shape[2]

    @pl.when(pl.program_id(0) == 0)
    def _():
        gram = gacc_ref[...] if has_acc else jnp.zeros(gram_ref.shape, jnp.float32)
        for rel in range(nz):
            value = freq_ref[rel]
            row = lax.rem(rel + pos_ref[1], nz) * chunk
            turned_ref[pl.ds(pl.multiple_of(row, chunk), chunk), :] = value.T.astype(jnp.bfloat16)
            gram += lax.dot_general(
                value, value, (((1,), (1,)), ((), ())), precision=HIGHEST,
                preferred_element_type=jnp.float32,
            )
        gram_ref[...] = gram

    part = jnp.dot(geno_ref[...], turned_ref[...], preferred_element_type=jnp.float32)
    value = part.T * 0.5
    out_ref[...] = acc_ref[...] + value if has_acc else value


def fit_part(freq, genotypes, group, z, groups, acc):
    nz, pops, chunk = freq.shape
    width = nz * chunk
    samples = genotypes.shape[0]
    if chunk % 128 or samples % 512:
        flat = jnp.transpose(jnp.roll(freq, z, axis=0), (1, 0, 2)).reshape(pops, width)
        cross = lax.dot_general(
            flat.astype(jnp.bfloat16),
            lax.dynamic_slice_in_dim(genotypes, group * width, width, 1),
            (((1,), (1,)), ((), ())),
            preferred_element_type=jnp.float32,
        )
        gram = jnp.dot(flat, flat.T, precision=HIGHEST)
        return (cross * 0.5, gram) if acc is None else (acc[0] + cross * 0.5, acc[1] + gram)
    rows = samples // 4
    out_specs = [
        pl.BlockSpec((pops, rows), lambda k, pos: (0, k)),
        pl.BlockSpec((pops, pops), lambda k, pos: (0, 0)),
    ]
    return pl.pallas_call(
        functools.partial(fit_kernel, nz, acc is not None),
        out_shape=[
            jax.ShapeDtypeStruct((pops, samples), jnp.float32),
            jax.ShapeDtypeStruct((pops, pops), jnp.float32),
        ],
        grid_spec=pltpu.PrefetchScalarGridSpec(
            num_scalar_prefetch=1,
            grid=(samples // rows,),
            in_specs=[
                pl.BlockSpec((nz, pops, chunk), lambda k, pos: (0, 0, 0)),
                pl.BlockSpec((rows, width), lambda k, pos: (k, pos[0])),
            ]
            + (out_specs if acc is not None else []),
            out_specs=out_specs,
            scratch_shapes=[pltpu.VMEM((width, pops), jnp.bfloat16)],
        ),
        cost_estimate=pl.CostEstimate(
            flops=2 * pops * samples * width, bytes_accessed=2 * samples * width, transcendentals=0
        ),
        compiler_params=pltpu.CompilerParams(vmem_limit_bytes=16 << 20),
        name="cross_q",
    )(jnp.stack([group, z]).astype(jnp.int32), freq, genotypes, *(acc or ()))


def inverse_kernel(*refs):
    *parts, out_ref = refs
    n = out_ref.shape[0]
    row_id = lax.broadcasted_iota(jnp.int32, (n, n), 0)
    col_id = lax.broadcasted_iota(jnp.int32, (n, n), 1)
    lane = lax.broadcasted_iota(jnp.int32, (1, n), 1)
    sub = lax.broadcasted_iota(jnp.int32, (n, 1), 0)
    a = parts[0][...]
    for ref in parts[1:]:
        a += ref[...]
    a += jnp.where(row_id == col_id, jnp.float32(RIDGE), jnp.float32(0))
    for k in range(n):
        pivot = 1.0 / a[k : k + 1, k : k + 1]
        row = jnp.where(lane == k, 1.0, a[k : k + 1, :]) * pivot
        col = jnp.where(sub == k, -1.0, a[:, k : k + 1])
        a = jnp.where((row_id == k) | (col_id == k), 0.0, a) - col * row
    out_ref[...] = a


def inverse(*parts):
    return pl.pallas_call(
        inverse_kernel,
        out_shape=jax.ShapeDtypeStruct(parts[0].shape, jnp.float32),
        cost_estimate=pl.CostEstimate(flops=1 << 23, bytes_accessed=1 << 22, transcendentals=64),
        compiler_params=pltpu.CompilerParams(vmem_limit_bytes=4 << 20),
        name="inverse",
    )(*parts)


def apply_kernel(inv_ref, *refs):
    *parts, out_ref = refs
    value = parts[0][...]
    for ref in parts[1:]:
        value += ref[...]
    out_ref[...] = jnp.dot(
        inv_ref[...], value, precision=HIGHEST, preferred_element_type=jnp.float32
    )


def apply_inverse(inv, *parts):
    return pl.pallas_call(
        apply_kernel,
        out_shape=jax.ShapeDtypeStruct(parts[0].shape, jnp.float32),
        cost_estimate=pl.CostEstimate(flops=1 << 21, bytes_accessed=1 << 20, transcendentals=0),
        compiler_params=pltpu.CompilerParams(vmem_limit_bytes=8 << 20),
        name="apply",
    )(inv, *parts)


def body(sizes, n_var, genotypes, start_q):
    nz, nx, nc = sizes
    groups = nx * nc
    me = lax.axis_index("samp")
    z, x, c = me // (nx * nc), (me // nc) % nx, me % nc

    def send(value, stage, shift):
        return lax.ppermute(value, "samp", shift_perm(sizes, stage, shift))

    def group_of(rc, rx):
        return (c + rc) % nc * nx + (x + rx) % nx

    def all_sum(value):
        for stage in (2, 1):
            value = functools.reduce(
                jnp.add, [send(value, stage, s) for s in range(1, sizes[stage])], value
            )
        return [value] + [send(value, 0, s) for s in range(1, nz)]

    ancestry = start_q
    for _ in range(ITERS):
        inv_q = inverse(*all_sum(jnp.dot(ancestry, ancestry.T, precision=HIGHEST)))
        order = [*range(1, nx), 0]
        arrived = {
            (rc, rx): send(
                cross_part(ancestry, genotypes, group_of(rc, rx), z, nz, groups), 2, rc
            )
            for rc in range(1, nc)
            for rx in order
        }
        kept = {
            rx: cross_part(
                ancestry, genotypes, group_of(0, rx), z, nz, groups,
                tuple(arrived[rc, rx] for rc in range(1, nc)),
            )
            for rx in order
        }
        mine = [kept[0]] + [send(kept[rx], 1, rx) for rx in range(1, nx)]
        chunks = [functools.reduce(jnp.add, [m[r] for m in mine]) for r in range(nz)]
        total = [chunks[0]] + [send(chunks[r], 0, r) for r in range(1, nz)]
        own = apply_inverse(inv_q, *total)

        held = {(0, 0): jnp.stack([own] + [send(own, 0, -r) for r in range(1, nz)])}
        for rx in range(1, nx):
            held[0, rx] = send(held[0, 0], 1, -rx)
        for rx in range(nx):
            for rc in range(1, nc):
                held[rc, rx] = send(held[0, rx], 2, -rc)

        acc = None
        for (rc, rx), freq in held.items():
            acc = fit_part(freq, genotypes, group_of(rc, rx), z, groups, acc)
        cross_q, gram_p = acc
        if n_var == 2:
            swap = [(0, 1), (1, 0)]
            gram_parts = [gram_p, lax.ppermute(gram_p, "var", swap)]
            cross_parts = [cross_q, lax.ppermute(cross_q, "var", swap)]
        else:
            gram_parts, cross_parts = [lax.psum(gram_p, "var")], [lax.psum(cross_q, "var")]
        ancestry = apply_inverse(inverse(*gram_parts), *cross_parts)

    chunk = own.shape[1]
    frequency = jnp.zeros((own.shape[0], genotypes.shape[1]), jnp.float32)
    for (rc, rx), freq in held.items():
        for r in range(nz):
            at = (group_of(rc, rx) * nz + (z + r) % nz) * chunk
            frequency = lax.dynamic_update_slice(frequency, freq[r], (0, at))
    return (ancestry, frequency)


def solution(mesh):
    sizes = split_samp(mesh.shape["samp"])
    return jax.shard_map(
        functools.partial(body, sizes, mesh.shape["var"]),
        mesh=mesh,
        in_specs=(P("samp", "var"), P(None, "samp")),
        out_specs=(P(None, "samp"), P(None, "var")),
        check_vma=False,
    )
```

```python
import functools

import jax
import jax.numpy as jnp
from jax import lax
from jax.experimental import pallas as pl
from jax.experimental.pallas import tpu as pltpu
from jax.sharding import PartitionSpec as P


ITERS = 2
RIDGE = 1.0
HIGHEST = lax.Precision.HIGHEST


def split_samp(n):
    core = 2 if n % 2 == 0 else 1
    rest = n // core
    inner = max(d for d in range(1, rest + 1) if rest % d == 0 and d * d <= rest)
    return rest // inner, inner, core


def shift_perm(sizes, stage, shift):
    nz, nx, nc = sizes
    pairs = []
    for z in range(nz):
        for x in range(nx):
            for c in range(nc):
                to = [z, x, c]
                to[stage] = (to[stage] + shift) % sizes[stage]
                pairs.append(((z * nx + x) * nc + c, (to[0] * nx + to[1]) * nc + to[2]))
    return pairs


def params(mib):
    return pltpu.CompilerParams(vmem_limit_bytes=mib << 20)


def cost(flops, read):
    return pl.CostEstimate(flops=flops, bytes_accessed=read, transcendentals=0)


VMEM = pl.BlockSpec(memory_space=pltpu.VMEM)
SMEM = pl.BlockSpec(memory_space=pltpu.SMEM)


def gram_of(value):
    high = value.astype(jnp.bfloat16)
    rest = value - high.astype(jnp.float32)
    middle = rest.astype(jnp.bfloat16)
    low = (rest - middle.astype(jnp.float32)).astype(jnp.bfloat16)
    pieces = jnp.concatenate([high, middle, low], axis=0)
    product = lax.dot_general(
        pieces, pieces, (((1,), (1,)), ((), ())), preferred_element_type=jnp.float32
    )
    n = value.shape[0]
    rows = product[2 * n :] + product[n : 2 * n] + product[:n]
    return rows[:, 2 * n :] + rows[:, n : 2 * n] + rows[:, :n]


def gram_kernel(value_ref, *refs):
    out_ref = refs[-1]
    if len(value_ref.shape) == 2:
        total = gram_of(value_ref[...])
    else:
        total = gram_of(jnp.concatenate([value_ref[r] for r in range(value_ref.shape[0])], axis=1))
    for ref in refs[:-1]:
        total += ref[...]
    out_ref[...] = total


def gram(value, *extra):
    pops, width = value.shape[-2:]
    if width % 128:
        flat = value if value.ndim == 2 else jnp.concatenate(list(value), axis=1)
        return functools.reduce(jnp.add, extra, jnp.dot(flat, flat.T, precision=HIGHEST))
    return pl.pallas_call(
        gram_kernel,
        out_shape=jax.ShapeDtypeStruct((pops, pops), jnp.float32),
        in_specs=[VMEM] * (1 + len(extra)),
        out_specs=VMEM,
        cost_estimate=cost(1 << 26, 1 << 20),
        compiler_params=params(8),
        name="gram",
    )(value, *extra)


def store_chunks(out_ref, value, z, nz, chunk, extra):
    for k in range(nz):
        rel = lax.rem(k - z + nz, nz)
        part = value[:, k * chunk : (k + 1) * chunk] * 0.5
        for ref in extra:
            part += ref[rel]
        out_ref[rel] = part


def cross_stream_kernel(nz, n_extra, pos_ref, anc_ref, geno_ref, *refs):
    extra, out_ref, acc_ref = refs[:n_extra], refs[n_extra], refs[n_extra + 1]
    step = pl.program_id(0)
    part = jnp.dot(
        anc_ref[...].astype(jnp.bfloat16), geno_ref[...], preferred_element_type=jnp.float32
    )

    @pl.when(step == 0)
    def _():
        acc_ref[...] = part

    @pl.when(step > 0)
    def _():
        acc_ref[...] += part

    @pl.when(step == pl.num_programs(0) - 1)
    def _():
        store_chunks(out_ref, acc_ref, pos_ref[0], nz, out_ref.shape[2], extra)


def cross_kernel(nz, at, n_extra, pos_ref, anc_ref, geno_ref, *refs):
    extra, out_ref = refs[:n_extra], refs[n_extra]
    chunk = out_ref.shape[2]
    width = nz * chunk
    ancestry_b = anc_ref[...].astype(jnp.bfloat16)
    first = pl.multiple_of(pos_ref[at] * width, 128)
    value = jnp.dot(
        ancestry_b, geno_ref[:, pl.ds(first, width)], preferred_element_type=jnp.float32
    )
    store_chunks(out_ref, value, pos_ref[0], nz, chunk, extra)


def aligned(chunk, samples):
    return chunk % 128 == 0 and samples % 512 == 0


def cross_part(ancestry, genotypes, pos, at, nz, groups, stream, extra=()):
    pops, samples = ancestry.shape
    width = genotypes.shape[1] // groups
    chunk = width // nz
    if not aligned(chunk, samples):
        part = jnp.dot(
            ancestry.astype(jnp.bfloat16),
            lax.dynamic_slice_in_dim(genotypes, pos[at] * width, width, 1),
            preferred_element_type=jnp.float32,
        )
        part = jnp.transpose((part * 0.5).reshape(pops, nz, chunk), (1, 0, 2))
        part = jnp.roll(part, -pos[0], axis=0)
        return functools.reduce(jnp.add, extra, part)
    out_shape = jax.ShapeDtypeStruct((nz, pops, chunk), jnp.float32)
    estimate = cost(2 * pops * samples * width, 2 * samples * width)
    if not stream:
        return pl.pallas_call(
            functools.partial(cross_kernel, nz, at, len(extra)),
            out_shape=out_shape,
            in_specs=[SMEM] + [VMEM] * (2 + len(extra)),
            out_specs=VMEM,
            cost_estimate=estimate,
            compiler_params=params(8),
            name="cross_p",
        )(pos, ancestry, genotypes, *extra)
    rows = samples // 4
    whole = pl.BlockSpec((nz, pops, chunk), lambda k, pos: (0, 0, 0))
    return pl.pallas_call(
        functools.partial(cross_stream_kernel, nz, len(extra)),
        out_shape=out_shape,
        grid_spec=pltpu.PrefetchScalarGridSpec(
            num_scalar_prefetch=1,
            grid=(samples // rows,),
            in_specs=[
                pl.BlockSpec((pops, rows), lambda k, pos: (0, k)),
                pl.BlockSpec((rows, width), lambda k, pos: (k, pos[at])),
            ]
            + [whole] * len(extra),
            out_specs=whole,
            scratch_shapes=[pltpu.VMEM((pops, width), jnp.float32)],
        ),
        cost_estimate=estimate,
        compiler_params=params(56),
        name="cross_p_stream",
    )(pos, ancestry, genotypes, *extra)


def fit_kernel(at, has_acc, last, pos_ref, freq_ref, geno_ref, *refs):
    out_ref, turned_ref = refs[-2:]
    nz, _, chunk = freq_ref.shape
    width = nz * chunk
    for rel in range(nz):
        row = lax.rem(rel + pos_ref[0], nz) * chunk
        turned_ref[pl.ds(pl.multiple_of(row, chunk), chunk), :] = freq_ref[rel].T.astype(
            jnp.bfloat16
        )
    first = pl.multiple_of(pos_ref[at] * width, 128)
    samples = geno_ref.shape[0]
    rows = samples // 4
    for k in range(4):
        part = slice(k * rows, (k + 1) * rows)
        value = 0.5 * jnp.dot(
            geno_ref[part, pl.ds(first, width)], turned_ref[...], preferred_element_type=jnp.float32
        )
        if has_acc:
            value += refs[0][part, :]
        if last:
            out_ref[:, part] = value.T
        else:
            out_ref[part, :] = value


def fit_part(freq, genotypes, pos, at, acc, last):
    nz, pops, chunk = freq.shape
    width = nz * chunk
    samples = genotypes.shape[0]
    if not aligned(chunk, samples):
        flat = jnp.transpose(jnp.roll(freq, pos[0], axis=0), (1, 0, 2)).reshape(pops, width)
        cross = 0.5 * lax.dot_general(
            flat.astype(jnp.bfloat16),
            lax.dynamic_slice_in_dim(genotypes, pos[at] * width, width, 1),
            (((1,), (1,)), ((), ())),
            preferred_element_type=jnp.float32,
        )
        return cross if acc is None else acc + cross
    extra = () if acc is None else (acc,)
    return pl.pallas_call(
        functools.partial(fit_kernel, at, acc is not None, last),
        out_shape=jax.ShapeDtypeStruct((pops, samples) if last else (samples, pops), jnp.float32),
        in_specs=[SMEM] + [VMEM] * (2 + len(extra)),
        out_specs=VMEM,
        scratch_shapes=[pltpu.VMEM((width, pops), jnp.bfloat16)],
        cost_estimate=cost(2 * pops * samples * width, 2 * samples * width),
        compiler_params=params(8),
        name="cross_q",
    )(pos, freq, genotypes, *extra)


def inverse_kernel(*refs):
    *parts, out_ref = refs
    n = out_ref.shape[0]
    row_id = lax.broadcasted_iota(jnp.int32, (n, n), 0)
    col_id = lax.broadcasted_iota(jnp.int32, (n, n), 1)
    lane = lax.broadcasted_iota(jnp.int32, (1, n), 1)
    sub = lax.broadcasted_iota(jnp.int32, (n, 1), 0)
    a = parts[0][...]
    for ref in parts[1:]:
        a += ref[...]
    a += jnp.where(row_id == col_id, jnp.float32(RIDGE), jnp.float32(0))
    for k in range(n):
        pivot = 1.0 / a[k : k + 1, k : k + 1]
        row = jnp.where(lane == k, 1.0, a[k : k + 1, :]) * pivot
        col = jnp.where(sub == k, -1.0, a[:, k : k + 1])
        a = jnp.where((row_id == k) | (col_id == k), 0.0, a) - col * row
    out_ref[...] = a


def inverse(*parts):
    return pl.pallas_call(
        inverse_kernel,
        out_shape=jax.ShapeDtypeStruct(parts[0].shape, jnp.float32),
        in_specs=[VMEM] * len(parts),
        out_specs=VMEM,
        cost_estimate=cost(1 << 28, 1 << 20),
        compiler_params=params(4),
        name="inverse",
    )(*parts)


def apply_kernel(inv_ref, *refs):
    *parts, out_ref = refs
    value = parts[0][...]
    for ref in parts[1:]:
        value += ref[...]
    out_ref[...] = jnp.dot(
        inv_ref[...], value, precision=HIGHEST, preferred_element_type=jnp.float32
    )


def apply_inverse(inv, *parts):
    return pl.pallas_call(
        apply_kernel,
        out_shape=jax.ShapeDtypeStruct(parts[0].shape, jnp.float32),
        in_specs=[VMEM] * (1 + len(parts)),
        out_specs=VMEM,
        cost_estimate=cost(1 << 21, 1 << 20),
        compiler_params=params(8),
        name="apply",
    )(inv, *parts)


def assemble_kernel(places, pos_ref, *refs):
    *held, out_ref = refs
    nz, _, chunk = held[0].shape
    for ref, at in zip(held, places):
        for r in range(nz):
            place = (pos_ref[at] * nz + lax.rem(pos_ref[0] + r, nz)) * chunk
            out_ref[:, pl.ds(pl.multiple_of(place, chunk), chunk)] = ref[r]


def assemble(held, pos, places):
    nz, pops, chunk = held[0].shape
    width = nz * chunk * len(held)
    if chunk % 128:
        frequency = jnp.zeros((pops, width), jnp.float32)
        for freq, at in zip(held, places):
            for r in range(nz):
                place = (pos[at] * nz + (pos[0] + r) % nz) * chunk
                frequency = lax.dynamic_update_slice(frequency, freq[r], (0, place))
        return frequency
    return pl.pallas_call(
        functools.partial(assemble_kernel, places),
        out_shape=jax.ShapeDtypeStruct((pops, width), jnp.float32),
        in_specs=[SMEM] + [VMEM] * len(held),
        out_specs=VMEM,
        cost_estimate=cost(1 << 20, 8 * pops * width),
        compiler_params=params(8),
        name="assemble",
    )(pos, *held)


def body(sizes, n_var, genotypes, start_q):
    nz, nx, nc = sizes
    groups = nx * nc
    me = lax.axis_index("samp")
    z, x, c = me // (nx * nc), (me // nc) % nx, me % nc
    pairs = [(rc, rx) for rx in range(nx) for rc in range(nc)]
    pos = jnp.stack([z] + [(c + rc) % nc * nx + (x + rx) % nx for rc, rx in pairs]).astype(jnp.int32)
    at = {pair: 1 + k for k, pair in enumerate(pairs)}

    def send(value, stage, shift):
        return lax.ppermute(value, "samp", shift_perm(sizes, stage, shift))

    ancestry = start_q
    for it in range(ITERS):
        total = gram(ancestry)
        for stage in (2, 1):
            total = functools.reduce(
                jnp.add, [send(total, stage, s) for s in range(1, sizes[stage])], total
            )
        gram_q = [total] + [send(total, 0, s) for s in range(1, nz)]
        inv_q = inverse(*gram_q)

        order = [*range(1, nx), 0]
        arrived = {}
        for rc in range(1, nc):
            for rx in order:
                part = cross_part(
                    ancestry, genotypes, pos, at[rc, rx], nz,
                    groups, it == 0,
                )
                arrived[rc, rx] = send(part, 2, rc)
        kept = {
            rx: cross_part(
                ancestry, genotypes, pos, at[0, rx], nz, groups,
                it == 0 and rx > 0, tuple(arrived[rc, rx] for rc in range(1, nc)),
            )
            for rx in order
        }
        mine = [kept[0]] + [send(kept[rx], 1, rx) for rx in range(1, nx)]
        chunks = [functools.reduce(jnp.add, [m[r] for m in mine]) for r in range(nz)]
        sums = [chunks[0]] + [send(chunks[r], 0, r) for r in range(1, nz)]
        own = apply_inverse(inv_q, *sums)

        held = {(0, 0): jnp.stack([own] + [send(own, 0, -r) for r in range(1, nz)])}
        for rx in range(1, nx):
            held[0, rx] = send(held[0, 0], 1, -rx)
        for rx in range(nx):
            for rc in range(1, nc):
                held[rc, rx] = send(held[0, rx], 2, -rc)

        gram_p, cross_q = (), None
        for pair in pairs:
            gram_p = (gram(held[pair], *gram_p),)
            cross_q = fit_part(
                held[pair], genotypes, pos, at[pair], cross_q,
                pair == pairs[-1],
            )
        gram_p = gram_p[0]
        if n_var == 2:
            swap = [(0, 1), (1, 0)]
            gram_parts = [gram_p, lax.ppermute(gram_p, "var", swap)]
            cross_parts = [cross_q, lax.ppermute(cross_q, "var", swap)]
        else:
            gram_parts, cross_parts = [lax.psum(gram_p, "var")], [lax.psum(cross_q, "var")]
        inv_p = inverse(*gram_parts)
        ancestry = apply_inverse(inv_p, *cross_parts)
        if it == ITERS - 1:
            frequency = assemble([held[p] for p in pairs], pos, [at[p] for p in pairs])
    return (ancestry, frequency)


def solution(mesh):
    sizes = split_samp(mesh.shape["samp"])
    return jax.shard_map(
        functools.partial(body, sizes, mesh.shape["var"]),
        mesh=mesh,
        in_specs=(P("samp", "var"), P(None, "samp")),
        out_specs=(P(None, "samp"), P(None, "var")),
        check_vma=False,
    )
```
